512 devices in a mesh: row: 32 (over y_hi, z), col: 16 (over x, y_lo, core).
Axes of the slice: x: 4, y: 4 (y_hi: 2, y_lo: 2; y = y_hi * 2 + y_lo), z: 16, core: 2. Of those that a mesh axis runs over, the one named last changes fastest.
Arguments:
- incoming_evolution_embedding: bfloat16 [64, 512, 64], P(None, 'row'), may hold values from -6 to 6
- learned_affine_stretch: float32 [64], replicated, may hold values from 0.5 to 1.5
- learned_affine_offset: float32 [64], replicated, may hold values from -3 to 3
- lefthand_mapping_tensor: bfloat16 [64, 32], replicated, may hold values from -0.75 to 0.75
- righthand_mapping_tensor: bfloat16 [64, 32], replicated, may hold values from -0.75 to 0.75
- final_outer_matrix: bfloat16 [1024, 128], replicated, may hold values from -0.1875 to 0.1875
- residue_couple_cotangent: bfloat16 [512, 512, 128], P('row', 'col'), may hold values from -6 to 6
Outputs:
- alignment_gradient: bfloat16 [64, 512, 64], P('col', 'row')
- left_weight_gradient: float32 [64, 32], replicated
- right_weight_gradient: float32 [64, 32], replicated
- output_weight_gradient: float32 [1024, 128], replicated
The draws below stay inside these ranges and needn't reach their ends.
All inputs are finite; a program needn't handle non-finite values.
Results may differ from the reference program's by a relative error of at most 0.0064.
Values may be sent and summed in bfloat16 or wider, within the bound.
No kernel may reach another device: no remote copies, remote signals or barrier semaphores. Data moves between devices by JAX's collectives and lax.ppermute only.
A program may use at most 64 MiB of HBM per device.

```python
import jax
import jax.numpy as jnp
from jax import lax

ENTRY_DEPTH = 64
HIDDEN_WIDTHS = 32
C_Z = 128
HOMOLOGS_STACKED = 64
TOK_R = 16
AMINO_SITES = 512
N_ROW = 32


def shard_levels(rng, extent, pieces, least, top_value):
    level, own = 1.0, jax.random.fold_in(rng, 6)
    for axis_at, parts in pieces:
        draws = jnp.exp(jax.random.uniform(jax.random.fold_in(own, axis_at), (parts,), jnp.float32, least / len(pieces), top_value / len(pieces)))
        level = level * jnp.repeat(draws, extent[axis_at] // parts).reshape([-1 if axis == axis_at else 1 for axis in range(len(extent))])
    return level


def gaussian(key, dims, spread, reach, pieces=(), kind=jnp.bfloat16):
    values = jax.random.normal(key, dims, jnp.float32) * spread
    if len(pieces) > 0:
        values = shard_levels(key, dims, pieces, -0.22, 0.18) * values
    return jnp.clip(values, min=-reach, max=reach).astype(kind)


def setup_inputs(seed: int = 0) -> dict:
    splits = jax.random.split(jax.random.key(seed), 8)
    incoming_evolution_embedding = gaussian(splits[0], (HOMOLOGS_STACKED, AMINO_SITES, ENTRY_DEPTH), 1.0, 6.0, ((1, 32),))
    learned_affine_stretch = jnp.clip(jax.random.uniform(splits[1], (ENTRY_DEPTH,), jnp.float32, 0.5, 1.5), 0.5, 1.5)
    learned_affine_offset = gaussian(splits[2], (ENTRY_DEPTH,), 0.5, 3.0, (), jnp.float32)
    lefthand_mapping_tensor = gaussian(splits[3], (ENTRY_DEPTH, HIDDEN_WIDTHS), ENTRY_DEPTH ** -0.5, 0.75)
    righthand_mapping_tensor = gaussian(splits[4], (ENTRY_DEPTH, HIDDEN_WIDTHS), ENTRY_DEPTH ** -0.5, 0.75)
    final_outer_matrix = gaussian(splits[5], (HIDDEN_WIDTHS * HIDDEN_WIDTHS, C_Z), (HIDDEN_WIDTHS * HIDDEN_WIDTHS) ** -0.5, 0.1875)
    residue_couple_cotangent = gaussian(splits[6], (AMINO_SITES, AMINO_SITES, C_Z), 1.0, 6.0, ((0, 32), (1, 16)))
    return {"incoming_evolution_embedding": incoming_evolution_embedding, "learned_affine_stretch": learned_affine_stretch, "learned_affine_offset": learned_affine_offset, "lefthand_mapping_tensor": lefthand_mapping_tensor, "righthand_mapping_tensor": righthand_mapping_tensor, "final_outer_matrix": final_outer_matrix, "residue_couple_cotangent": residue_couple_cotangent}


highest = lax.Precision.HIGHEST

def standardize_features(values, learned_affine_stretch, learned_affine_offset):
    values = values.astype(jnp.float32)
    mean_value = lax.optimization_barrier(jnp.mean(values, -1, keepdims=True))
    centred = values - mean_value
    variance = lax.optimization_barrier(jnp.mean(centred * centred, -1, keepdims=True))
    reciprocal_spread_std = lax.rsqrt(variance + 1e-05)
    multiplied_activations = centred * reciprocal_spread_std
    standardized_activations = (multiplied_activations * learned_affine_stretch + learned_affine_offset).astype(jnp.bfloat16)
    return (multiplied_activations, reciprocal_spread_std, standardized_activations)

def project(standardized_activations, weight):
    array_shape = standardized_activations.shape
    flat = jnp.dot(standardized_activations.reshape(-1, array_shape[-1]), weight, preferred_element_type=jnp.float32)
    return flat.astype(jnp.bfloat16).reshape(array_shape[:-1] + (weight.shape[1],))

def outer_block(left_block, right_matrix, grad_block, final_outer_matrix, element_number, hidden):
    rows = grad_block.shape[0]
    cols = grad_block.shape[1]
    outer = lax.dot_general(left_block, right_matrix, (((0,), (0,)), ((), ())), preferred_element_type=jnp.float32)
    outer = (outer * (1.0 / element_number)).astype(jnp.bfloat16)
    outer = outer.reshape(rows, hidden, cols, hidden).transpose(0, 2, 1, 3).reshape(rows * cols, hidden * hidden)
    flat_grad = grad_block.reshape(rows * cols, grad_block.shape[2])
    weight_term = lax.dot_general(outer, flat_grad, (((0,), (0,)), ((), ())), preferred_element_type=jnp.float32)
    outer_grad = lax.dot_general(flat_grad, final_outer_matrix, (((1,), (1,)), ((), ())), preferred_element_type=jnp.float32)
    outer_grad = outer_grad.astype(jnp.bfloat16)
    outer_grad = outer_grad.reshape(rows, cols, hidden, hidden).transpose(0, 2, 1, 3).reshape(rows * hidden, cols * hidden)
    left_term = lax.dot_general(outer_grad, right_matrix, (((1,), (1,)), ((), ())), preferred_element_type=jnp.float32)
    left_term = (left_term * (1.0 / element_number)).reshape(rows, hidden, element_number).transpose(2, 0, 1)
    right_term = jnp.dot(left_block, outer_grad, preferred_element_type=jnp.float32) * (1.0 / element_number)
    return (weight_term, left_term, right_term)

def norm_gradient_pass(left_gradient, right_gradient, lefthand_mapping_tensor, righthand_mapping_tensor, multiplied_activations, reciprocal_spread_std, learned_affine_stretch):
    hidden = lefthand_mapping_tensor.shape[1]
    hidden_grad = jnp.dot(left_gradient.reshape(-1, hidden), lefthand_mapping_tensor.astype(jnp.float32).T, precision=highest)
    hidden_grad = hidden_grad + jnp.dot(right_gradient.reshape(-1, hidden), righthand_mapping_tensor.astype(jnp.float32).T, precision=highest)
    hidden_grad = hidden_grad.reshape(multiplied_activations.shape) * learned_affine_stretch
    mean_one = lax.optimization_barrier(jnp.mean(hidden_grad, -1, keepdims=True))
    mean_two = lax.optimization_barrier(jnp.mean(hidden_grad * multiplied_activations, -1, keepdims=True))
    return (reciprocal_spread_std * (hidden_grad - mean_one - multiplied_activations * mean_two)).astype(jnp.bfloat16)

def weight_grad(standardized_activations, factor_grad):
    feature_width = standardized_activations.shape[-1]
    hidden = factor_grad.shape[-1]
    return lax.dot_general(standardized_activations.astype(jnp.float32).reshape(-1, feature_width), factor_grad.reshape(-1, hidden), (((0,), (0,)), ((), ())), precision=highest, preferred_element_type=jnp.float32)

def reference(incoming_evolution_embedding, learned_affine_stretch, learned_affine_offset, lefthand_mapping_tensor, righthand_mapping_tensor, final_outer_matrix, residue_couple_cotangent):
    element_number = incoming_evolution_embedding.shape[0]
    hidden = lefthand_mapping_tensor.shape[1]
    multiplied_activations, reciprocal_spread_std, standardized_activations = standardize_features(incoming_evolution_embedding, learned_affine_stretch, learned_affine_offset)
    left_factor = project(standardized_activations, lefthand_mapping_tensor)
    right_factor = project(standardized_activations, righthand_mapping_tensor)
    right_matrix = right_factor.reshape(element_number, AMINO_SITES * hidden)

    def visit(carry, index):
        weight_acc, right_acc = carry
        offset = index * TOK_R
        left_block = lax.dynamic_slice_in_dim(left_factor, offset, TOK_R, 1).reshape(element_number, TOK_R * hidden)
        grad_block = lax.dynamic_slice_in_dim(residue_couple_cotangent, offset, TOK_R, 0)
        weight_term, left_term, right_term = outer_block(left_block, right_matrix, grad_block, final_outer_matrix, element_number, hidden)
        return ((weight_acc + weight_term, right_acc + right_term), left_term)
    init = (jnp.zeros((hidden * hidden, C_Z), jnp.float32), jnp.zeros((element_number, AMINO_SITES * hidden), jnp.float32))
    (weight_sum, right_sum), left_parts = lax.scan(visit, init, jnp.arange(N_ROW, dtype=jnp.int32))
    left_gradient = left_parts.transpose(1, 0, 2, 3).reshape(element_number, AMINO_SITES, hidden)
    right_gradient = right_sum.reshape(element_number, AMINO_SITES, hidden)
    alignment_gradient = norm_gradient_pass(left_gradient, right_gradient, lefthand_mapping_tensor, righthand_mapping_tensor, multiplied_activations, reciprocal_spread_std, learned_affine_stretch)
    left_weight_gradient = weight_grad(standardized_activations, left_gradient) * (1.0 / AMINO_SITES)
    right_weight_gradient = weight_grad(standardized_activations, right_gradient) * (1.0 / AMINO_SITES)
    output_weight_gradient = weight_sum * (1.0 / AMINO_SITES)
    return (alignment_gradient, left_weight_gradient, right_weight_gradient, output_weight_gradient)
```

```python
import math

import jax
import jax.numpy as jnp
from jax import lax
from jax.sharding import PartitionSpec as P

highest = lax.Precision.HIGHEST


def swap_pairs(rows, cols, turn):
    ratio = rows // cols
    return [
        (
            source * cols + copy,
            (ratio * copy + (source + turn) % ratio) * cols + source // ratio,
        )
        for source in range(rows)
        for copy in range(cols)
    ]


def home_pairs(rows, cols):
    ratio = rows // cols
    return [
        ((half * cols + share) * cols + col, (ratio * col + half) * cols + share)
        for half in range(ratio)
        for share in range(cols)
        for col in range(cols)
    ]


def swap_tokens(own, row_index, rows, cols):
    ratio = rows // cols
    arrived = [
        lax.ppermute(own, ("row", "col"), swap_pairs(rows, cols, turn)) for turn in range(ratio)
    ]
    ordered = []
    for part in range(ratio):
        chosen = arrived[0]
        for turn in range(1, ratio):
            chosen = jnp.where((row_index - turn) % ratio == part, arrived[turn], chosen)
        ordered.append(chosen)
    return ordered


def trade(pieces, axis):
    return lax.all_to_all(pieces, axis, 0, 0, tiled=True)


def spread(piece, axis):
    extent = lax.axis_size(axis)
    return trade(jnp.broadcast_to(piece[None], (extent,) + piece.shape), axis)


def standardize_features(values, learned_affine_stretch, learned_affine_offset):
    values = values.astype(jnp.float32)
    mean_value = jnp.mean(values, -1, keepdims=True)
    centred = values - mean_value
    variance = jnp.mean(centred * centred, -1, keepdims=True)
    reciprocal_spread_std = lax.rsqrt(variance + 1e-05)
    multiplied_activations = centred * reciprocal_spread_std
    standardized_activations = (
        multiplied_activations * learned_affine_stretch + learned_affine_offset
    ).astype(jnp.bfloat16)
    return (multiplied_activations, reciprocal_spread_std, standardized_activations)


def project(standardized_activations, weight):
    array_shape = standardized_activations.shape
    flat = jnp.dot(
        standardized_activations.reshape(-1, array_shape[-1]),
        weight,
        preferred_element_type=jnp.float32,
    )
    return flat.astype(jnp.bfloat16).reshape(array_shape[:-1] + (weight.shape[1],))


def outer_block(left_block, right_matrix, grad_block, final_outer_matrix, element_number, hidden):
    rows = grad_block.shape[0]
    cols = grad_block.shape[1]
    outer = lax.dot_general(
        left_block, right_matrix, (((0,), (0,)), ((), ())), preferred_element_type=jnp.float32
    )
    outer = (outer * (1.0 / element_number)).astype(jnp.bfloat16)
    outer = (
        outer.reshape(rows, hidden, cols, hidden)
        .transpose(0, 2, 1, 3)
        .reshape(rows * cols, hidden * hidden)
    )
    flat_grad = grad_block.reshape(rows * cols, grad_block.shape[2])
    weight_term = lax.dot_general(
        outer, flat_grad, (((0,), (0,)), ((), ())), preferred_element_type=jnp.float32
    )
    outer_grad = lax.dot_general(
        flat_grad, final_outer_matrix, (((1,), (1,)), ((), ())), preferred_element_type=jnp.float32
    )
    outer_grad = outer_grad.astype(jnp.bfloat16)
    outer_grad = (
        outer_grad.reshape(rows, cols, hidden, hidden)
        .transpose(0, 2, 1, 3)
        .reshape(rows * hidden, cols * hidden)
    )
    left_term = lax.dot_general(
        outer_grad, right_matrix, (((1,), (1,)), ((), ())), preferred_element_type=jnp.float32
    )
    left_term = (
        (left_term * (1.0 / element_number))
        .reshape(rows, hidden, element_number)
        .transpose(2, 0, 1)
    )
    right_term = jnp.dot(left_block, outer_grad, preferred_element_type=jnp.float32) * (
        1.0 / element_number
    )
    return (weight_term, left_term, right_term)


def norm_gradient_pass(
    left_gradient,
    right_gradient,
    lefthand_mapping_tensor,
    righthand_mapping_tensor,
    multiplied_activations,
    reciprocal_spread_std,
    learned_affine_stretch,
):
    hidden = lefthand_mapping_tensor.shape[1]
    hidden_grad = jnp.dot(
        left_gradient.reshape(-1, hidden),
        lefthand_mapping_tensor.astype(jnp.float32).T,
        precision=highest,
    )
    hidden_grad = hidden_grad + jnp.dot(
        right_gradient.reshape(-1, hidden),
        righthand_mapping_tensor.astype(jnp.float32).T,
        precision=highest,
    )
    hidden_grad = hidden_grad.reshape(multiplied_activations.shape) * learned_affine_stretch
    mean_one = jnp.mean(hidden_grad, -1, keepdims=True)
    mean_two = jnp.mean(hidden_grad * multiplied_activations, -1, keepdims=True)
    return (
        reciprocal_spread_std * (hidden_grad - mean_one - multiplied_activations * mean_two)
    ).astype(jnp.bfloat16)


def weight_grad(standardized_activations, factor_grad):
    feature_width = standardized_activations.shape[-1]
    hidden = factor_grad.shape[-1]
    return lax.dot_general(
        standardized_activations.astype(jnp.float32).reshape(-1, feature_width),
        factor_grad.reshape(-1, hidden),
        (((0,), (0,)), ((), ())),
        precision=highest,
        preferred_element_type=jnp.float32,
    )


def on_device(
    incoming_evolution_embedding,
    learned_affine_stretch,
    learned_affine_offset,
    lefthand_mapping_tensor,
    righthand_mapping_tensor,
    final_outer_matrix,
    residue_couple_cotangent,
):
    homolog_number, residue_slices, feature_width = incoming_evolution_embedding.shape
    hidden = lefthand_mapping_tensor.shape[1]
    pair_width = final_outer_matrix.shape[1]
    rows, cols = lax.axis_size("row"), lax.axis_size("col")
    ratio = rows // cols
    residue_position = lax.axis_index("col")
    row_index = lax.axis_index("row")
    multiplied_activations, reciprocal_spread_std, standardized_activations = standardize_features(
        incoming_evolution_embedding, learned_affine_stretch, learned_affine_offset
    )
    right_own = project(standardized_activations, righthand_mapping_tensor)
    right_parts = swap_tokens(
        right_own.reshape(homolog_number, residue_slices * hidden), row_index, rows, cols
    )
    right_matrix = jnp.concatenate(right_parts, 1)
    left_factor = project(standardized_activations, lefthand_mapping_tensor)
    tok_cols = ratio * residue_slices
    block_rows = math.gcd(residue_slices, 8)
    weight_acc = jnp.zeros((hidden * hidden, pair_width), jnp.float32)
    right_acc = jnp.zeros((homolog_number, tok_cols * hidden), jnp.float32)
    left_parts = []
    for offset in range(0, residue_slices, block_rows):
        left_block = left_factor[:, offset : offset + block_rows, :].reshape(
            homolog_number, block_rows * hidden
        )
        grad_block = residue_couple_cotangent[offset : offset + block_rows]
        weight_term, left_term, right_term = outer_block(
            left_block, right_matrix, grad_block, final_outer_matrix, homolog_number, hidden
        )
        weight_acc = weight_acc + weight_term
        right_acc = right_acc + right_term
        left_parts.append(left_term)
    left_partial = jnp.concatenate(left_parts, 1)

    seq_share = homolog_number // cols
    seq_first = residue_position * seq_share
    chunk = (seq_share * residue_slices * hidden // pair_width, pair_width)
    right_pieces = (
        right_acc.astype(jnp.bfloat16)
        .reshape(cols, seq_share, ratio, residue_slices * hidden)
        .transpose(2, 0, 1, 3)
        .reshape((rows,) + chunk)
    )
    left_pieces = left_partial.astype(jnp.bfloat16).reshape((cols,) + chunk)
    weight_pieces = weight_acc.astype(jnp.bfloat16).reshape(cols, -1, pair_width)
    col_taken = trade(jnp.concatenate([left_pieces, weight_pieces], 1), "col")
    row_taken = trade(right_pieces, "row")
    right_sum = jnp.sum(row_taken.astype(jnp.float32), 0)
    right_sum = lax.ppermute(right_sum, ("row", "col"), home_pairs(rows, cols))
    col_sum = jnp.sum(col_taken.astype(jnp.float32), 0)
    own_shape = (seq_share, residue_slices, hidden)
    left_gradient = col_sum[: chunk[0]].reshape(own_shape)
    right_gradient = right_sum.reshape(own_shape)
    weight_share = col_sum[chunk[0] :]

    scaled_own_part = lax.dynamic_slice_in_dim(multiplied_activations, seq_first, seq_share, 0)
    inverse_own_scale = lax.dynamic_slice_in_dim(reciprocal_spread_std, seq_first, seq_share, 0)
    normed_own = lax.dynamic_slice_in_dim(standardized_activations, seq_first, seq_share, 0)
    both_weight = weight_grad(
        normed_own, jnp.concatenate([left_gradient, right_gradient], -1)
    ).reshape(rows, -1, pair_width)
    weight_rows = weight_share.shape[0] // rows
    row_pieces = jnp.concatenate(
        [weight_share.reshape(rows, weight_rows, pair_width), both_weight], 1
    )
    row_sum = jnp.sum(trade(row_pieces, "row"), 0)
    gathered = spread(row_sum, "row")
    weight_full = gathered[:, :weight_rows].reshape(-1, pair_width)
    both_part = gathered[:, weight_rows:].reshape(-1, pair_width)
    last = spread(jnp.concatenate([weight_full, both_part], 0).astype(jnp.bfloat16), "col")
    last = last.astype(jnp.float32)
    tokens = residue_slices * rows
    output_weight = last[:, : weight_full.shape[0]].reshape(-1, pair_width) * (1.0 / tokens)
    both_total = jnp.sum(last[:, weight_full.shape[0] :], 0) * (1.0 / tokens)
    both_total = both_total.reshape(feature_width, 2 * hidden)
    alignment_gradient = norm_gradient_pass(
        left_gradient,
        right_gradient,
        lefthand_mapping_tensor,
        righthand_mapping_tensor,
        scaled_own_part,
        inverse_own_scale,
        learned_affine_stretch,
    )
    return (alignment_gradient, both_total[:, :hidden], both_total[:, hidden:], output_weight)


def solution(mesh):
    in_specs = (P(None, "row", None), P(), P(), P(), P(), P(), P("row", "col", None))
    out_specs = (P("col", "row", None), P(), P(), P())
    return jax.shard_map(
        on_device, mesh=mesh, in_specs=in_specs, out_specs=out_specs, check_vma=False
    )
```

```python
import functools

import jax
import jax.numpy as jnp
from jax import lax
from jax.experimental import pallas as pl
from jax.experimental.pallas import tpu as pltpu
from jax.sharding import PartitionSpec as P

highest = lax.Precision.HIGHEST
LANES = 128
SUBLANES = 8


def swap_pairs(rows, cols, turn):
    ratio = rows // cols
    return [
        (
            source * cols + copy,
            (ratio * copy + (source + turn) % ratio) * cols + source // ratio,
        )
        for source in range(rows)
        for copy in range(cols)
    ]


def home_pairs(rows, cols):
    ratio = rows // cols
    return [
        ((half * cols + share) * cols + col, (ratio * col + half) * cols + share)
        for half in range(ratio)
        for share in range(cols)
        for col in range(cols)
    ]


def trade(pieces, axis):
    return lax.all_to_all(pieces, axis, 0, 0, tiled=True)


def spread(piece, axis):
    extent = lax.axis_size(axis)
    return trade(jnp.broadcast_to(piece[None], (extent,) + piece.shape), axis)


def factor_kernel(
    values_ref,
    stretch_ref,
    offset_ref,
    left_map_ref,
    right_map_ref,
    left_ref,
    right_ref,
    normed_own_ref,
    scaled_own_ref,
    inverse_own_ref,
    normed_ref,
    *,
    shares,
):
    homologs, tokens, width = values_ref.shape
    hidden = left_map_ref.shape[1]
    seq_share = homologs // shares
    values = values_ref[...].astype(jnp.float32)
    mean_value = jnp.mean(values, -1, keepdims=True)
    centred = values - mean_value
    variance = jnp.mean(centred * centred, -1, keepdims=True)
    inverse = lax.rsqrt(variance + 1e-05)
    scaled = centred * inverse
    normed = scaled * stretch_ref[...][None] + offset_ref[...][None]
    normed = normed.astype(jnp.bfloat16).astype(jnp.float32)
    normed_ref[...] = normed.reshape(homologs * tokens, width)

    own = pl.ds(lax.axis_index("col") * seq_share, seq_share)
    own_values = values_ref[own].astype(jnp.float32)
    own_centred = own_values - jnp.mean(own_values, -1, keepdims=True)
    own_inverse = lax.rsqrt(jnp.mean(own_centred * own_centred, -1, keepdims=True) + 1e-05)
    own_scaled = own_centred * own_inverse
    scaled_own_ref[...] = own_scaled
    inverse_own_ref[...] = jnp.broadcast_to(own_inverse, own_scaled.shape)
    normed_own_ref[...] = (own_scaled * stretch_ref[...][None] + offset_ref[...][None]).astype(
        jnp.bfloat16
    )

    maps = jnp.concatenate(
        [left_map_ref[...].astype(jnp.float32).T, right_map_ref[...].astype(jnp.float32).T], 0
    ).astype(jnp.bfloat16)
    for pair in range(tokens // 2):
        block = jnp.concatenate(
            [
                normed_ref[pl.ds((s4 * tokens) + t1 * (tokens // 2) + pair, shares, stride=seq_share * tokens), :]
                for t1 in range(2)
                for s4 in range(seq_share)
            ],
            0,
        ).astype(jnp.bfloat16)
        both = lax.dot_general(
            maps, block, (((1,), (1,)), ((), ())), preferred_element_type=jnp.float32
        ).astype(jnp.bfloat16)
        quad, place = pair // 2, pair % 2
        left_ref[quad * hidden : (quad + 1) * hidden, place * LANES : (place + 1) * LANES] = both[
            :hidden
        ]
        right_ref[pair * hidden : (pair + 1) * hidden, :] = both[hidden:]


def quad_tokens(quad, tokens):
    return [t1 * (tokens // 2) + 2 * quad + place for place in range(2) for t1 in range(2)]


def grad_kernel(
    left_ref, matrix_ref, cotangent_ref, outer_grad_ref, right_out_ref, wide_ref, sum_ref, *, shares
):
    tokens, columns, width = cotangent_ref.shape
    quads = tokens // 4
    hidden = left_ref.shape[0] // quads
    homologs = left_ref.shape[1] // 4
    wide_ref[...] = matrix_ref[...].astype(jnp.float32)
    by_right = jnp.concatenate(
        [wide_ref[pl.ds(e, hidden, stride=hidden), :] for e in range(hidden)], 0
    ).astype(jnp.bfloat16)
    for quad in range(quads):
        block = jnp.concatenate([cotangent_ref[t] for t in quad_tokens(quad, tokens)], 0)
        product = lax.dot_general(
            by_right, block, (((1,), (1,)), ((), ())), preferred_element_type=jnp.float32
        ).astype(jnp.bfloat16)
        for e in range(hidden):
            outer_grad_ref[
                quad * hidden : (quad + 1) * hidden, e * LANES : (e + 1) * LANES
            ] = product[e * hidden : (e + 1) * hidden]

    turned = left_ref[...].astype(jnp.float32).T.astype(jnp.bfloat16)
    lane = lax.broadcasted_iota(jnp.int32, (homologs, LANES), 1)
    quarter = lane // columns
    even = (lane // (columns // 2)) % 2 == 0
    for group in range(hidden // 8):
        product = jnp.dot(
            turned,
            outer_grad_ref[:, group * 8 * LANES : (group + 1) * 8 * LANES],
            preferred_element_type=jnp.float32,
        )
        packed = [None, None]
        for e in range(8):
            part = product[:homologs, e * LANES : (e + 1) * LANES]
            for place in range(1, 4):
                part = jnp.where(
                    quarter == place,
                    product[place * homologs : (place + 1) * homologs, e * LANES : (e + 1) * LANES],
                    part,
                )
            part = part + pltpu.roll(part, LANES // 2, 1)
            part = part + pltpu.roll(part, LANES // 4, 1)
            which, place = e % 2, e // 2
            packed[which] = (
                part if place == 0 else jnp.where(quarter == place, part, packed[which])
            )
        first = jnp.where(even, packed[0], pltpu.roll(packed[1], columns // 2, 1))
        second = jnp.where(even, pltpu.roll(packed[0], LANES - columns // 2, 1), packed[1])
        scale = 1.0 / homologs
        sum_ref[0, group * homologs : (group + 1) * homologs, :] = first * scale
        sum_ref[1, group * homologs : (group + 1) * homologs, :] = second * scale
    for half in range(2):
        for share in range(shares):
            right_out_ref[half * shares + share] = sum_ref[
                half, pl.ds(share, right_out_ref.shape[1], stride=shares), :
            ].astype(jnp.bfloat16)


def pair_kernel(
    left_ref,
    first_ref,
    second_ref,
    outer_grad_ref,
    cotangent_ref,
    out_ref,
    half_ref,
    block_ref,
    outer_ref,
    turn_ref,
):
    tokens, columns, width = cotangent_ref.shape
    quads = tokens // 4
    hidden = left_ref.shape[0] // quads
    homologs = left_ref.shape[1] // 4
    scale = 1.0 / homologs
    shares, share_rows = out_ref.shape[0], turn_ref.shape[0] // out_ref.shape[0]
    straight = lax.axis_index("row") % 2 == 0
    first = first_ref[...].astype(jnp.float32)
    second = second_ref[...].astype(jnp.float32)
    half_ref[0] = jnp.where(straight, first, second)
    half_ref[1] = jnp.where(straight, second, first)
    low = lax.broadcasted_iota(jnp.int32, (SUBLANES, LANES), 1) < LANES // 2
    zero = jnp.zeros((SUBLANES, LANES), jnp.float32)
    block_ref[...] = jnp.zeros_like(block_ref)
    for e in range(hidden):
        lows, highs = [], []
        for half in range(2):
            part = half_ref[half, pl.ds(e, SUBLANES, stride=hidden), :]
            turned = pltpu.roll(part, LANES // 2, 1)
            lows += [jnp.where(low, part, zero), jnp.where(low, turned, zero)]
            highs += [jnp.where(low, zero, turned), jnp.where(low, zero, part)]
        lows = jnp.concatenate(lows, 0).astype(jnp.bfloat16)
        highs = jnp.concatenate(highs, 0).astype(jnp.bfloat16)
        base = e * LANES
        for place in range(4):
            block_ref[
                base + place * columns : base + (place + 1) * columns,
                place // 2 * LANES : (place // 2 + 1) * LANES,
            ] = lows if place % 2 == 0 else highs

    left = left_ref[...]
    for group in range(hidden // 8):
        outer = lax.dot_general(
            left,
            block_ref[group * 8 * LANES : (group + 1) * 8 * LANES, :],
            (((1,), (1,)), ((), ())),
            preferred_element_type=jnp.float32,
        )
        outer = (outer * scale).astype(jnp.bfloat16)
        for step in range(8):
            e = group * 8 + step
            for quad in range(quads):
                outer_ref[
                    e * hidden : (e + 1) * hidden, quad * LANES : (quad + 1) * LANES
                ] = outer[quad * hidden : (quad + 1) * hidden, step * LANES : (step + 1) * LANES]
    cotangent = jnp.concatenate(
        [cotangent_ref[t] for quad in range(quads) for t in quad_tokens(quad, tokens)], 0
    )
    weight_rows = out_ref.shape[1] - share_rows
    for share in range(shares):
        out_ref[share, share_rows:, :] = jnp.dot(
            outer_ref[share * weight_rows : (share + 1) * weight_rows, :],
            cotangent,
            preferred_element_type=jnp.float32,
        ).astype(jnp.bfloat16)
    left_part = jnp.dot(
        outer_grad_ref[...], block_ref[...], preferred_element_type=jnp.float32
    )
    turn_ref[...] = (left_part * scale).T
    for share in range(shares):
        out_ref[share, :share_rows, :] = turn_ref[
            pl.ds(share, share_rows, stride=shares), :
        ].astype(jnp.bfloat16)


def vmem(count):
    return [pl.BlockSpec(memory_space=pltpu.VMEM)] * count


def norm_gradient_pass(
    left_gradient,
    right_gradient,
    lefthand_mapping_tensor,
    righthand_mapping_tensor,
    multiplied_activations,
    reciprocal_spread_std,
    learned_affine_stretch,
):
    hidden = lefthand_mapping_tensor.shape[1]
    both = jnp.concatenate([left_gradient, right_gradient], -1).reshape(-1, 2 * hidden)
    maps = jnp.concatenate([lefthand_mapping_tensor, righthand_mapping_tensor], 1)
    hidden_grad = jnp.dot(both, maps.astype(jnp.float32).T, precision=highest)
    hidden_grad = hidden_grad.reshape(multiplied_activations.shape) * learned_affine_stretch
    mean_one = jnp.mean(hidden_grad, -1, keepdims=True)
    mean_two = jnp.mean(hidden_grad * multiplied_activations, -1, keepdims=True)
    return (
        reciprocal_spread_std * (hidden_grad - mean_one - multiplied_activations * mean_two)
    ).astype(jnp.bfloat16)


def weight_grad(standardized_activations, factor_grad):
    feature_width = standardized_activations.shape[-1]
    hidden = factor_grad.shape[-1]
    return lax.dot_general(
        standardized_activations.astype(jnp.float32).reshape(-1, feature_width),
        factor_grad.reshape(-1, hidden),
        (((0,), (0,)), ((), ())),
        precision=highest,
        preferred_element_type=jnp.float32,
    )


def on_device(
    incoming_evolution_embedding,
    learned_affine_stretch,
    learned_affine_offset,
    lefthand_mapping_tensor,
    righthand_mapping_tensor,
    final_outer_matrix,
    residue_couple_cotangent,
):
    homologs, tokens, width = incoming_evolution_embedding.shape
    hidden = lefthand_mapping_tensor.shape[1]
    pair_width = final_outer_matrix.shape[1]
    columns = residue_couple_cotangent.shape[1]
    rows, cols = lax.axis_size("row"), lax.axis_size("col")
    seq_share = homologs // cols
    quads = tokens // 4
    everywhere = ("row", "col")
    bf16, f32 = jnp.bfloat16, jnp.float32
    left, right, normed_own, scaled_own, inverse_own = pl.pallas_call(
        functools.partial(factor_kernel, shares=cols),
        out_shape=[
            jax.ShapeDtypeStruct((quads * hidden, 4 * homologs), bf16),
            jax.ShapeDtypeStruct((tokens // 2 * hidden, 2 * homologs), bf16),
            jax.ShapeDtypeStruct((seq_share, tokens, width), bf16),
            jax.ShapeDtypeStruct((seq_share, tokens, width), f32),
            jax.ShapeDtypeStruct((seq_share, tokens, width), f32),
        ],
        in_specs=vmem(5),
        out_specs=vmem(5),
        scratch_shapes=[pltpu.VMEM((homologs * tokens, width), f32)],
        cost_estimate=pl.CostEstimate(flops=10_000_000, bytes_accessed=400_000, transcendentals=0),
        name="factors",
    )(
        incoming_evolution_embedding,
        learned_affine_stretch.reshape(1, width),
        learned_affine_offset.reshape(1, width),
        lefthand_mapping_tensor,
        righthand_mapping_tensor,
    )
    first = lax.ppermute(right, everywhere, swap_pairs(rows, cols, 0))
    second = lax.ppermute(right, everywhere, swap_pairs(rows, cols, 1))
    home = home_pairs(rows, cols)
    normed_away = lax.ppermute(normed_own, everywhere, [(b, a) for a, b in home])
    outer_grad, right_pieces = pl.pallas_call(
        functools.partial(grad_kernel, shares=cols),
        out_shape=[
            jax.ShapeDtypeStruct((quads * hidden, hidden * LANES), bf16),
            jax.ShapeDtypeStruct((rows, hidden // 8 * seq_share, LANES), bf16),
        ],
        in_specs=vmem(3),
        out_specs=vmem(2),
        scratch_shapes=[
            pltpu.VMEM((hidden * hidden, pair_width), f32),
            pltpu.VMEM((2, hidden // 8 * homologs, LANES), f32),
        ],
        cost_estimate=pl.CostEstimate(
            flops=800_000_000, bytes_accessed=2_000_000, transcendentals=0
        ),
        name="grads",
    )(left, final_outer_matrix, residue_couple_cotangent)
    row_taken = trade(right_pieces, "row")
    share_rows = 4 * seq_share
    weight_share_rows = hidden * hidden // cols
    col_pieces = pl.pallas_call(
        pair_kernel,
        out_shape=jax.ShapeDtypeStruct((cols, share_rows + weight_share_rows, LANES), bf16),
        in_specs=vmem(5),
        out_specs=vmem(1)[0],
        scratch_shapes=[
            pltpu.VMEM((2, tokens // 2 * hidden, 2 * homologs), f32),
            pltpu.VMEM((hidden * LANES, 4 * homologs), bf16),
            pltpu.VMEM((hidden * hidden, quads * LANES), bf16),
            pltpu.VMEM((4 * homologs, quads * hidden), f32),
        ],
        cost_estimate=pl.CostEstimate(
            flops=1_200_000_000, bytes_accessed=2_000_000, transcendentals=0
        ),
        name="pairs",
    )(left, first, second, outer_grad, residue_couple_cotangent)
    col_taken = trade(col_pieces, "col")

    right_sum = jnp.sum(row_taken.astype(f32), 0)
    right_home = lax.ppermute(right_sum, everywhere, home)

    def right_order(summed):
        summed = summed.reshape(hidden // 8, seq_share, 8, tokens).transpose(1, 3, 0, 2)
        return summed.reshape(seq_share, tokens, hidden)

    right_weight = weight_grad(normed_away, right_order(right_sum))
    col_sum = jnp.sum(col_taken.astype(f32), 0)
    left_gradient = (
        col_sum[:share_rows]
        .reshape(2, 2, seq_share, quads, hidden)
        .transpose(2, 1, 3, 0, 4)
        .reshape(seq_share, tokens, hidden)
    )
    left_weight = weight_grad(normed_own, left_gradient)
    both_weight = jnp.concatenate([left_weight, right_weight], 1).reshape(rows, -1, pair_width)
    weight_rows = weight_share_rows // rows
    row_pieces = jnp.concatenate(
        [col_sum[share_rows:].reshape(rows, weight_rows, pair_width), both_weight], 1
    )
    row_sum = jnp.sum(trade(row_pieces.astype(bf16), "row").astype(f32), 0)
    gathered = spread(row_sum.astype(bf16), "row")
    weight_full = gathered[:, :weight_rows].reshape(-1, pair_width)
    both_part = gathered[:, weight_rows:].reshape(-1, pair_width)
    last = spread(jnp.concatenate([weight_full, both_part], 0), "col").astype(f32)
    inverse_tokens = 1.0 / (tokens * rows)
    output_weight = (
        (last[:, :weight_share_rows] * inverse_tokens)
        .reshape(hidden, hidden, pair_width)
        .transpose(1, 0, 2)
        .reshape(hidden * hidden, pair_width)
    )
    both_total = jnp.sum(last[:, weight_share_rows:], 0) * inverse_tokens
    both_total = both_total.reshape(width, 2 * hidden)
    alignment_gradient = norm_gradient_pass(
        left_gradient,
        right_order(right_home),
        lefthand_mapping_tensor,
        righthand_mapping_tensor,
        scaled_own,
        inverse_own,
        learned_affine_stretch,
    )
    return (alignment_gradient, both_total[:, :hidden], both_total[:, hidden:], output_weight)


def solution(mesh):
    in_specs = (P(None, "row", None), P(), P(), P(), P(), P(), P("row", "col", None))
    out_specs = (P("col", "row", None), P(), P(), P())
    return jax.shard_map(
        on_device, mesh=mesh, in_specs=in_specs, out_specs=out_specs, check_vma=False
    )
```
